32 devices in a mesh: dp: 16 (over z, y, core), shard: 2 (over x).
Axes of the slice: x: 2, y: 2, z: 4, core: 2. Of those that a mesh axis runs over, the one named last changes fastest.
Arguments:
- fast_weights: float32 [16, 1280, 3072], P('dp', None, 'shard'), may hold values from -6 to 6
- gradient: bfloat16 [16, 1280, 3072], P('dp', None, 'shard'), may hold values from -6 to 6
- first_moment: float32 [16, 1280, 3072], P('dp', None, 'shard'), may hold values from -0.6 to 0.6
- second_moment: float32 [16, 1280, 3072], P('dp', None, 'shard'), may hold values from 0.0001 to 1
- slow_weights: float32 [1280, 3072], P('dp', 'shard'), may hold values from -6 to 6
Outputs:
- fresh_weights: float32 [1280, 3072], P(None, 'shard')
- slow_synced: float32 [1280, 3072], P('dp', 'shard')
- new_first: float32 [16, 1280, 3072], P('dp', None, 'shard')
- new_second: float32 [16, 1280, 3072], P('dp', None, 'shard')
The draws below stay inside these ranges and needn't reach their ends.
All inputs are finite; a program needn't handle non-finite values.
Results may differ from the reference program's by a relative error of at most 0.0003.
Values sent between devices are 32-bit elements; how exact they have to be, the bound alone decides.
A program may use at most 128 MiB of HBM per device.

```python
import math
import jax
import jax.numpy as jnp
from jax import lax

D = 1280
FFW = 3072
GROUPS = 16
N_DP = 16


def with_spikes(array, own_key, source, target, shards_of, factor):
    owner, partner = [(jnp.arange(array.shape[dim]) // (array.shape[dim] // shards_of)).reshape([-1 if axis == dim else 1 for axis in range(array.ndim)]) for dim in (source, target)]
    chosen = jax.random.permutation(own_key, shards_of)[partner]
    strong = (owner == chosen) | (owner == (partner + shards_of // 2) % shards_of)
    return jnp.where(strong, factor * array, array)


def shard_levels(own_key, extent, pieces, low, high):
    factor_of, own = 1.0, jax.random.fold_in(own_key, 6)
    for axis_at, shards_of in pieces:
        heights = jnp.exp(jax.random.uniform(jax.random.fold_in(own, axis_at), (shards_of,), jnp.float32, low / len(pieces), high / len(pieces)))
        factor_of = factor_of * jnp.repeat(heights, extent[axis_at] // shards_of).reshape([-1 if axis == axis_at else 1 for axis in range(len(extent))])
    return factor_of


def gaussian(rng, extent, deviation, most, split=(), kind=jnp.bfloat16):
    factor_of = shard_levels(rng, extent, split, -0.22, 0.18) if split else 1.0
    array = jax.random.normal(rng, extent, jnp.float32) * deviation * factor_of
    return jnp.minimum(jnp.maximum(array, -most), most).astype(kind)


def bell_draw_with(key, dims, width, limit, cuts, heavy, dtype=jnp.bfloat16):
    entries = width * jax.random.normal(key, dims, jnp.float32)
    if cuts:
        entries = entries * shard_levels(key, dims, cuts, -0.22, 0.18)
    return jnp.clip(with_spikes(entries, jax.random.fold_in(key, 3), *heavy), -limit, limit).astype(dtype)


def setup_inputs(seed: int = 0) -> dict:
    keys = jax.random.split(jax.random.key(seed), 6)
    return {
        "fast_weights": bell_draw_with(keys[0], (GROUPS, D, FFW), 1.0, 6.0, ((0, 16), (2, 2)), (0, 1, 16, 2.0), jnp.float32),
        "gradient": gaussian(keys[1], (GROUPS, D, FFW), 1.0, 6.0, ((0, 16), (2, 2))),
        "first_moment": gaussian(keys[2], (GROUPS, D, FFW), 0.1, 0.6, ((0, 16), (2, 2)), jnp.float32),
        "second_moment": jnp.clip(jnp.exp(math.log(1.0) - 9.2103404 * jax.random.uniform(keys[3], (GROUPS, D, FFW), jnp.float32) ** shard_levels(keys[3], (GROUPS, D, FFW), ((0, 16), (2, 2)), -0.2, 0.2)), 0.0001, 1.0),
        "slow_weights": gaussian(keys[4], (D, FFW), 1.0, 6.0, ((0, 16), (1, 2)), jnp.float32),
    }


beta_first = 0.9
beta_second = 0.999
learning_rate = 0.01
weight_decay = 0.05
epsilon = 1e-08
blend_rate = 0.5
first_bias = 1.0 - 0.9 ** 5
second_bias = 1.0 - 0.999 ** 5

def reference(fast_weights, gradient, first_moment, second_moment, slow_weights):
    grad_value = gradient.astype(jnp.float32)
    new_first = beta_first * first_moment + (1.0 - beta_first) * grad_value
    new_second = beta_second * second_moment + (1.0 - beta_second) * grad_value * grad_value
    direction = new_first / first_bias / (jnp.sqrt(new_second / second_bias) + epsilon)
    stepped = fast_weights - learning_rate * (direction + weight_decay * fast_weights)
    average = lax.optimization_barrier(jnp.sum(stepped, axis=0)) / N_DP
    slow_synced = slow_weights + blend_rate * (average - slow_weights)
    return (slow_synced, slow_synced, new_first, new_second)
```

```python
import functools
import heapq

import jax
import jax.numpy as jnp
from jax import lax
from jax.experimental import pallas as pl
from jax.experimental.pallas import tpu as pltpu
from jax.sharding import PartitionSpec as P

beta_first = 0.9
beta_second = 0.999
learning_rate = 0.01
weight_decay = 0.05
epsilon = 1e-08
blend_rate = 0.5
first_bias = 1.0 - 0.9**5
second_bias = 1.0 - 0.999**5


def plan(n, chunks):
    bits = n.bit_length() - 1
    inner = (bits - 1) // 2
    near = list(range(1, 1 + inner))
    far = list(range(1 + inner, bits))
    usual = [0] + near + far
    other = [0] + far[:1] + near + far[1:]
    orders = [other if k % 4 == 1 else usual for k in range(chunks)]
    link = {b: 0 if b == 0 else 1 if b in near else 2 for b in range(bits)}
    rate = {0: 6.0, 1: 1.0, 2: 1.0}
    free = {0: 0.0, 1: 0.0, 2: 0.0}
    events, arrivals = [], []

    def start(now, k, s):
        step = s if s < bits else 2 * bits - 1 - s
        b = orders[k][step]
        size = 64.0 / chunks / 2 ** (step + 1)
        begin = max(now, free[link[b]])
        free[link[b]] = begin + size / rate[link[b]]
        heapq.heappush(events, (free[link[b]] + 1.5, k, s))

    for k in range(chunks):
        start(0.0, k, 0)
    while events:
        now, k, s = heapq.heappop(events)
        arrivals.append((k, s))
        if s + 1 < 2 * bits:
            start(now + 0.3, k, s + 1)
    return orders, arrivals


def sync_kernel(n, chunks, orders, arrivals, x_ref, slow_ref, fresh_ref, synced_ref, *scratch):
    bits = n.bit_length() - 1
    parts = scratch[:bits]
    landed = scratch[bits : 2 * bits]
    gathered, send_sem, recv_sem = scratch[2 * bits :]
    width = x_ref.shape[-1] // chunks
    me = lax.axis_index("dp")
    bit = [(me // 2**b) % 2 for b in range(bits)]
    partner = [me + 2**b - 2 * 2**b * bit[b] for b in range(bits)]

    barrier = pltpu.get_barrier_semaphore()
    for b in range(bits):
        pl.semaphore_signal(barrier, inc=1, device_id={"dp": partner[b]}, device_id_type=pl.DeviceIdType.MESH)
    pl.semaphore_wait(barrier, bits)

    def columns(k):
        return pl.ds(k * width, width)

    def offset(k, depth):
        at = 0
        for s in range(1, depth):
            at = at + bit[orders[k][s]] * (n >> (s + 1))
        return at

    def place(k, block):
        at = 0
        for s in range(1, bits):
            at += ((block >> (orders[k][s] - 1)) & 1) * (n >> (s + 1))
        return at

    def copy(k, s):
        if s < bits:
            b = orders[k][s]
            if s == 0:
                src = x_ref.at[:, 1 - bit[0], :, columns(k)]
            else:
                half = n >> (s + 1)
                src = parts[s - 1].at[k, pl.ds((1 - bit[b]) * half, half)]
            dst = landed[s].at[k]
        else:
            step = 2 * bits - 1 - s
            b = orders[k][step]
            if step == 0:
                src = dst = fresh_ref.at[:, bit[0], :, columns(k)]
            else:
                src = dst = gathered.at[k, pl.ds(offset(k, step + 1), n >> (step + 1))]
        return pltpu.make_async_remote_copy(
            src_ref=src,
            dst_ref=dst,
            send_sem=send_sem.at[k, s],
            recv_sem=recv_sem.at[k, s],
            device_id={"dp": partner[b]},
            device_id_type=pl.DeviceIdType.MESH,
        )

    for k in range(chunks):
        copy(k, 0).start()

    for k, s in arrivals:
        copy(k, s).wait_recv()
        if s == 0:
            for block in range(n // 2):
                parts[0][k, place(k, block)] = x_ref[block, bit[0], :, columns(k)] + landed[0][k, block]
        elif s < bits:
            half = n >> (s + 1)
            mine = bit[orders[k][s]] * half
            for block in range(half):
                parts[s][k, block] = parts[s - 1][k, mine + block] + landed[s][k, block]
        if s == bits - 1:
            average = parts[s][k, 0] / n
            slow = slow_ref[:, columns(k)]
            synced = slow + blend_rate * (average - slow)
            synced_ref[:, columns(k)] = synced
            gathered[k, offset(k, bits)] = synced
        if s == 2 * bits - 2:
            for block in range(n // 2):
                fresh_ref[block, bit[0], :, columns(k)] = gathered[k, place(k, block)]
        if s + 1 < 2 * bits:
            copy(k, s + 1).start()

    for k in range(chunks):
        for s in range(2 * bits):
            copy(k, s).wait_send()


def synchronise(n, stepped, slow_weights):
    rows, cols = stepped.shape
    own = rows // n
    width = 256 if cols % 256 == 0 else 128
    chunks = cols // width
    bits = n.bit_length() - 1
    orders, arrivals = plan(n, chunks)
    f32 = jnp.float32
    fresh, synced = pl.pallas_call(
        functools.partial(sync_kernel, n, chunks, orders, arrivals),
        out_shape=(
            jax.ShapeDtypeStruct((n // 2, 2, own, cols), f32),
            jax.ShapeDtypeStruct((own, cols), f32),
        ),
        in_specs=[pl.BlockSpec(memory_space=pltpu.VMEM)] * 2,
        out_specs=[pl.BlockSpec(memory_space=pltpu.VMEM)] * 2,
        scratch_shapes=[
            *[pltpu.VMEM((chunks, n >> (s + 1), own, width), f32) for s in range(bits)],
            *[pltpu.VMEM((chunks, n >> (s + 1), own, width), f32) for s in range(bits)],
            pltpu.VMEM((chunks, n // 2, own, width), f32),
            pltpu.SemaphoreType.DMA((chunks, 2 * bits)),
            pltpu.SemaphoreType.DMA((chunks, 2 * bits)),
        ],
        compiler_params=pltpu.CompilerParams(
            collective_id=0, has_side_effects=True, vmem_limit_bytes=56 * 2**20
        ),
        name="sync",
    )(stepped.reshape(n // 2, 2, own, cols), slow_weights)
    return fresh.reshape(rows, cols), synced


def local(n, fast_weights, gradient, first_moment, second_moment, slow_weights):
    grad_value = gradient.astype(jnp.float32)
    new_first = beta_first * first_moment + (1.0 - beta_first) * grad_value
    new_second = beta_second * second_moment + (1.0 - beta_second) * grad_value * grad_value
    direction = new_first / first_bias / (jnp.sqrt(new_second / second_bias) + epsilon)
    stepped = fast_weights - learning_rate * (direction + weight_decay * fast_weights)
    fresh_weights, slow_synced = synchronise(n, stepped[0], slow_weights)
    return (fresh_weights, slow_synced, new_first, new_second)


def solution(mesh):
    return jax.shard_map(
        functools.partial(local, mesh.shape["dp"]),
        mesh=mesh,
        in_specs=(
            P("dp", None, "shard"),
            P("dp", None, "shard"),
            P("dp", None, "shard"),
            P("dp", None, "shard"),
            P("dp", "shard"),
        ),
        out_specs=(
            P(None, "shard"),
            P("dp", "shard"),
            P("dp", None, "shard"),
            P("dp", None, "shard"),
        ),
        check_vma=False,
    )
```

```python
import functools
import heapq

import jax
import jax.numpy as jnp
from jax import lax
from jax.experimental import pallas as pl
from jax.experimental.pallas import tpu as pltpu
from jax.sharding import PartitionSpec as P

beta_first = 0.9
beta_second = 0.999
learning_rate = 0.01
weight_decay = 0.05
epsilon = 1e-08
blend_rate = 0.5
first_bias = 1.0 - 0.9**5
second_bias = 1.0 - 0.999**5


def grid_of(n):
    chips = n // 2
    fast = 2 ** ((chips.bit_length() - 1) // 2)
    return chips // fast, fast


def plan(n, chunks):
    slow, fast = grid_of(n)
    orders = [((0, slow), (1, fast)) if (k + 1) * 5 // 12 > k * 5 // 12 else ((1, fast), (0, slow)) for k in range(chunks)]
    free, queued, events, arrivals = {}, {}, [], []

    def send(now, link, units):
        free[link] = max(now, free.get(link, 0.0)) + units * (0.15 if link == "core" else 0.9)
        return free[link]

    def line_of(k, stage):
        at = stage - 1 if stage < 3 else 4 - stage
        return orders[k][at] + (orders[k][1][1] if at == 0 else 1,)

    def start(now, k, stage, tick):
        if stage in (0, 5):
            done = send(now, "core", n // 2)
        else:
            axis, length, units = line_of(k, stage)
            if stage < 3:
                if tick == 0:
                    queued[k, stage] = [send(now, (axis, 0), units) for _ in range(length - 1)]
                ends = [queued[k, stage][tick]] + [send(now, (axis, i), units) for i in range(1, tick + 1)]
            else:
                ends = [send(now, (axis, i), units) for i in range(tick, length - 1)]
            done = max(ends)
        heapq.heappush(events, (done + 1.8, k, stage, tick))

    for k in range(chunks):
        start(0.3 * k, k, 0, 0)
    while events:
        now, k, stage, tick = heapq.heappop(events)
        arrivals.append((k, stage, tick))
        last = stage in (0, 5) or tick == line_of(k, stage)[1] - 2
        if not last:
            start(now + 0.1, k, stage, tick + 1)
        elif stage < 5:
            start(now + 0.2, k, stage + 1, 0)
    return orders, arrivals


def sync_kernel(n, chunks, orders, arrivals, x_hbm, slow_ref, fresh_ref, synced_ref, *scratch):
    x_ref, load_sem, send_sem, recv_sem = scratch[:4]
    buffers = [scratch[4 + 6 * k : 10 + 6 * k] for k in range(chunks)]
    width = x_ref.shape[-1] // chunks
    slow, fast = grid_of(n)
    me = lax.axis_index("dp")
    core = me % 2
    places = (me // (2 * fast), (me // 2) % fast)
    strides = (2 * fast, 2)
    other = me + 1 - 2 * core

    def columns(k):
        return pl.ds(k * width, width)

    def load(k):
        return pltpu.make_async_copy(x_hbm.at[:, :, :, columns(k)], x_ref.at[:, :, :, columns(k)], load_sem.at[k])

    for k in range(chunks):
        load(k).start()

    barrier = pltpu.get_barrier_semaphore()

    def greet(device):
        pl.semaphore_signal(barrier, inc=1, device_id={"dp": device}, device_id_type=pl.DeviceIdType.MESH)

    greet(other)
    peers = 1
    for axis, length in enumerate((slow, fast)):
        below, above = places[axis] > 0, places[axis] < length - 1
        pl.when(below)(functools.partial(greet, me - strides[axis]))
        pl.when(above)(functools.partial(greet, me + strides[axis]))
        peers = peers + jnp.where(below, 1, 0) + jnp.where(above, 1, 0)
    pl.semaphore_wait(barrier, peers)

    def copy(k, stage, tick, way, src, dst, device):
        return pltpu.make_async_remote_copy(
            src_ref=src,
            dst_ref=dst,
            send_sem=send_sem.at[k, stage, tick, way],
            recv_sem=recv_sem.at[k, stage, tick, way],
            device_id={"dp": device},
            device_id_type=pl.DeviceIdType.MESH,
        )

    def core_copy(k, stage):
        if stage == 0:
            src, dst = x_ref.at[:, 1 - core, :, columns(k)], buffers[k][0]
        else:
            src = dst = fresh_ref.at[:, core, :, columns(k)]
        return copy(k, stage, 0, 0, src, dst, other)

    class Line:
        def __init__(self, k, stage):
            at = stage - 1 if stage < 3 else 4 - stage
            self.k, self.stage = k, stage
            axis, self.length = orders[k][at]
            self.place = places[axis]
            self.units = orders[k][1][1] if at == 0 else 1
            self.step = strides[axis]
            landed0, sums, landed1, middle, landed2, gathered = buffers[k]
            self.source = sums if at == 0 else middle
            self.landed = landed1 if at == 0 else landed2
            self.gathered = gathered
            self.base = 0 if at == 0 else places[orders[k][0][0]] * orders[k][1][1]

        def far(self, way):
            return self.place if way == 0 else self.length - 1 - self.place

        def real(self, way, block):
            return block if way == 0 else self.length - 1 - block

        def block(self, way, block):
            return pl.ds(self.real(way, block) * self.units, self.units)

        def held(self, way, block):
            return self.gathered.at[pl.ds(self.base + self.real(way, block) * self.units, self.units)]

        def next(self, way):
            return me + self.step if way == 0 else me - self.step

        def copy(self, tick, way, src, dst):
            return copy(self.k, self.stage, tick, way, src, dst, self.next(way))

        def arrived(self, tick, way):
            if self.stage < 3:
                ref = self.landed.at[way, tick]
            else:
                ref = self.held(way, self.far(way) - 1 - tick)
            self.copy(tick, way, ref, ref).wait_recv()

        def begin(self):
            for way in (0, 1):
                far = self.far(way)
                if self.stage < 3:

                    @pl.when(far == 0)
                    def _():
                        for tick in range(self.length - 1):
                            src = self.source.at[self.block(way, self.length - 1 - tick)]
                            self.copy(tick, way, src, self.landed.at[way, tick]).start()
                else:

                    @pl.when(far < self.length - 1)
                    def _():
                        own = self.held(way, far)
                        self.copy(0, way, own, own).start()

        def reduce(self, tick, out):
            last = self.length - 2
            if tick < last:
                for way in (0, 1):
                    far = self.far(way)

                    @pl.when((far >= 1) & (far <= tick + 1))
                    def _():
                        self.arrived(tick, way)
                        here = self.landed.at[way, tick]
                        here[...] += self.source[self.block(way, last - tick + far)]
                        self.copy(tick + 1, way, here, self.landed.at[way, tick + 1]).start()
                return
            mine = pl.ds(self.place * self.units, self.units)

            @pl.when(self.place == 0)
            def _():
                self.arrived(last, 1)
                out[...] = self.source[mine] + self.landed[1, last]

            @pl.when(self.place == self.length - 1)
            def _():
                self.arrived(last, 0)
                out[...] = self.source[mine] + self.landed[0, last]

            if self.length > 2:

                @pl.when((self.place > 0) & (self.place < self.length - 1))
                def _():
                    self.arrived(last, 0)
                    self.arrived(last, 1)
                    out[...] = self.source[mine] + self.landed[0, last] + self.landed[1, last]

        def gather(self, tick):
            for way in (0, 1):
                far = self.far(way)

                @pl.when(far >= 1 + tick)
                def _():
                    self.arrived(tick, way)
                    if tick < self.length - 2:

                        @pl.when(far < self.length - 1)
                        def _():
                            got = self.held(way, far - 1 - tick)
                            self.copy(tick + 1, way, got, got).start()

        def sent(self):
            for way in (0, 1):
                far = self.far(way)
                for tick in range(self.length - 1):
                    if self.stage < 3:
                        ref, did = self.landed.at[way, tick], far <= tick
                    else:
                        ref, did = self.held(way, far - tick), far >= tick

                    @pl.when(did & (far < self.length - 1))
                    def _():
                        self.copy(tick, way, ref, ref).wait_send()

    def position(k, pair):
        where = (pair // fast, pair % fast)
        (first, _), (second, length) = orders[k]
        return where[first] * length + where[second]

    for k in range(chunks):
        load(k).wait()
        core_copy(k, 0).start()

    for k, stage, tick in arrivals:
        landed0, sums, landed1, middle, landed2, gathered = buffers[k]
        if stage == 0:
            core_copy(k, 0).wait_recv()
            for pair in range(n // 2):
                sums[position(k, pair)] = x_ref[pair, core, :, columns(k)] + landed0[pair]
            Line(k, 1).begin()
        elif stage == 5:
            core_copy(k, 5).wait_recv()
        else:
            line = Line(k, stage)
            last = tick == line.length - 2
            if stage == 1:
                line.reduce(tick, middle)
            elif stage == 2:
                own = gathered.at[pl.ds(line.base + line.place, 1)]
                line.reduce(tick, own)
                if last:
                    average = own[0] / n
                    slow_part = slow_ref[:, columns(k)]
                    synced = slow_part + blend_rate * (average - slow_part)
                    synced_ref[:, columns(k)] = synced
                    own[0] = synced
            else:
                line.gather(tick)
            if last and stage < 4:
                Line(k, stage + 1).begin()
            elif last:
                for pair in range(n // 2):
                    fresh_ref[pair, core, :, columns(k)] = gathered[position(k, pair)]
                core_copy(k, 5).start()

    for k in range(chunks):
        core_copy(k, 0).wait_send()
        for stage in (1, 2, 3, 4):
            Line(k, stage).sent()
        core_copy(k, 5).wait_send()


def synchronise(n, stepped, slow_weights):
    rows, cols = stepped.shape
    own = rows // n
    width = 128
    chunks = cols // width
    orders, arrivals = plan(n, chunks)
    slow, fast = grid_of(n)
    ticks = max(slow, fast) - 1
    f32 = jnp.float32
    buffers = []
    for (_, first), (_, second) in orders:
        buffers += [
            pltpu.VMEM((n // 2, own, width), f32),
            pltpu.VMEM((n // 2, own, width), f32),
            pltpu.VMEM((2, first - 1, second, own, width), f32),
            pltpu.VMEM((second, own, width), f32),
            pltpu.VMEM((2, second - 1, 1, own, width), f32),
            pltpu.VMEM((n // 2, own, width), f32),
        ]
    fresh, synced = pl.pallas_call(
        functools.partial(sync_kernel, n, chunks, orders, arrivals),
        out_shape=(
            pltpu.VMEM((n // 2, 2, own, cols), f32),
            jax.ShapeDtypeStruct((own, cols), f32),
        ),
        in_specs=[pl.BlockSpec(memory_space=pl.ANY), pl.BlockSpec(memory_space=pltpu.VMEM)],
        out_specs=[pl.BlockSpec(memory_space=pltpu.VMEM)] * 2,
        scratch_shapes=[
            pltpu.VMEM((n // 2, 2, own, cols), f32),
            pltpu.SemaphoreType.DMA((chunks,)),
            pltpu.SemaphoreType.DMA((chunks, 6, ticks, 2)),
            pltpu.SemaphoreType.DMA((chunks, 6, ticks, 2)),
            *buffers,
        ],
        compiler_params=pltpu.CompilerParams(
            collective_id=0, has_side_effects=True, vmem_limit_bytes=48 * 2**20
        ),
        name="sync",
    )(stepped.reshape(n // 2, 2, own, cols), slow_weights)
    return fresh.reshape(rows, cols), synced


def local(n, fast_weights, gradient, first_moment, second_moment, slow_weights):
    grad_value = gradient.astype(jnp.float32)
    new_first = beta_first * first_moment + (1.0 - beta_first) * grad_value
    new_second = beta_second * second_moment + (1.0 - beta_second) * grad_value * grad_value
    direction = new_first / first_bias / (jnp.sqrt(new_second / second_bias) + epsilon)
    stepped = fast_weights - learning_rate * (direction + weight_decay * fast_weights)
    fresh_weights, slow_synced = synchronise(n, stepped[0], slow_weights)
    return (fresh_weights, slow_synced, new_first, new_second)


def solution(mesh):
    return jax.shard_map(
        functools.partial(local, mesh.shape["dp"]),
        mesh=mesh,
        in_specs=(
            P("dp", None, "shard"),
            P("dp", None, "shard"),
            P("dp", None, "shard"),
            P("dp", None, "shard"),
            P("dp", "shard"),
        ),
        out_specs=(
            P(None, "shard"),
            P("dp", "shard"),
            P("dp", None, "shard"),
            P("dp", None, "shard"),
        ),
        check_vma=False,
    )
```

```python
import functools
import heapq

import jax
import jax.numpy as jnp
from jax import lax
from jax.experimental import pallas as pl
from jax.experimental.pallas import tpu as pltpu
from jax.sharding import PartitionSpec as P

beta_first = 0.9
beta_second = 0.999
learning_rate = 0.01
weight_decay = 0.05
epsilon = 1e-08
blend_rate = 0.5
first_bias = 1.0 - 0.9**5
second_bias = 1.0 - 0.999**5


def grid_of(n):
    chips = n // 2
    fast = 2 ** ((chips.bit_length() - 1) // 2)
    return chips // fast, fast


def plan(n, chunks):
    slow, fast = grid_of(n)
    orders = [((1, fast), (0, slow))] * chunks
    free, queued, events, arrivals = {}, {}, [], []

    def send(now, link, units):
        free[link] = max(now, free.get(link, 0.0)) + units * (0.15 if link == "core" else 0.9)
        return free[link]

    def line_of(k, stage):
        at = stage - 1 if stage < 3 else 4 - stage
        return orders[k][at] + (orders[k][1][1] if at == 0 else 1,)

    def start(now, k, stage, tick):
        if stage in (0, 5):
            done = send(now, "core", n // 2)
        else:
            axis, length, units = line_of(k, stage)
            if stage < 3:
                if tick == 0:
                    queued[k, stage] = [send(now, (axis, 0), units) for _ in range(length - 1)]
                ends = [queued[k, stage][tick]] + [send(now, (axis, i), units) for i in range(1, tick + 1)]
            else:
                ends = [send(now, (axis, i), units) for i in range(tick, length - 1)]
            done = max(ends)
        heapq.heappush(events, (done + 1.8, k, stage, tick))

    for k in range(chunks):
        heapq.heappush(events, (2.0 + 1.0 * k, k, -1, 0))
    while events:
        now, k, stage, tick = heapq.heappop(events)
        arrivals.append((k, stage, tick))
        last = stage in (-1, 0, 5) or tick == line_of(k, stage)[1] - 2
        if not last:
            start(now + 0.1, k, stage, tick + 1)
        elif stage < 5:
            start(now + 0.2, k, stage + 1, 0)
    return orders, arrivals


def sync_kernel(n, chunks, orders, arrivals, fast_hbm, grad_hbm, first_hbm, second_hbm, slow_ref, fresh_ref, synced_ref, first_ref, second_ref, *scratch):
    x_ref, grad_ref, load_sem, send_sem, recv_sem = scratch[:5]
    buffers = [scratch[5 + 6 * k : 11 + 6 * k] for k in range(chunks)]
    width = x_ref.shape[-1] // chunks
    slow, fast = grid_of(n)
    me = lax.axis_index("dp")
    core = me % 2
    places = (me // (2 * fast), (me // 2) % fast)
    strides = (2 * fast, 2)
    other = me + 1 - 2 * core

    def columns(k):
        return pl.ds(k * width, width)

    pairs = ((grad_hbm, grad_ref), (first_hbm, first_ref), (second_hbm, second_ref), (fast_hbm, x_ref))

    def loads(k):
        return [
            pltpu.make_async_copy(src.at[:, :, :, columns(k)], dst.at[:, :, :, columns(k)], load_sem.at[k, i])
            for i, (src, dst) in enumerate(pairs)
        ]

    def adam(k):
        @pl.loop(0, n)
        def _(block):
            at = (block // 2, block % 2, slice(None), columns(k))
            grad_value = grad_ref[at].astype(jnp.float32)
            new_first = beta_first * first_ref[at] + (1.0 - beta_first) * grad_value
            new_second = beta_second * second_ref[at] + (1.0 - beta_second) * grad_value * grad_value
            first_ref[at] = new_first
            second_ref[at] = new_second
            direction = new_first / first_bias / (jnp.sqrt(new_second / second_bias) + epsilon)
            weights = x_ref[at]
            x_ref[at] = weights - learning_rate * (direction + weight_decay * weights)

    for k in range(chunks):
        for load in loads(k):
            load.start()

    barrier = pltpu.get_barrier_semaphore()

    def greet(device):
        pl.semaphore_signal(barrier, inc=1, device_id={"dp": device}, device_id_type=pl.DeviceIdType.MESH)

    greet(other)
    peers = 1
    for axis, length in enumerate((slow, fast)):
        below, above = places[axis] > 0, places[axis] < length - 1
        pl.when(below)(functools.partial(greet, me - strides[axis]))
        pl.when(above)(functools.partial(greet, me + strides[axis]))
        peers = peers + jnp.where(below, 1, 0) + jnp.where(above, 1, 0)
    pl.semaphore_wait(barrier, peers)

    def copy(k, stage, tick, way, src, dst, device):
        return pltpu.make_async_remote_copy(
            src_ref=src,
            dst_ref=dst,
            send_sem=send_sem.at[k, stage, tick, way],
            recv_sem=recv_sem.at[k, stage, tick, way],
            device_id={"dp": device},
            device_id_type=pl.DeviceIdType.MESH,
        )

    def core_copy(k, stage):
        if stage == 0:
            src, dst = x_ref.at[:, 1 - core, :, columns(k)], buffers[k][0]
        else:
            src = dst = fresh_ref.at[:, core, :, columns(k)]
        return copy(k, stage, 0, 0, src, dst, other)

    class Line:
        def __init__(self, k, stage):
            at = stage - 1 if stage < 3 else 4 - stage
            self.k, self.stage = k, stage
            axis, self.length = orders[k][at]
            self.place = places[axis]
            self.units = orders[k][1][1] if at == 0 else 1
            self.step = strides[axis]
            landed0, sums, landed1, middle, landed2, gathered = buffers[k]
            self.source = sums if at == 0 else middle
            self.landed = landed1 if at == 0 else landed2
            self.gathered = gathered
            self.base = 0 if at == 0 else places[orders[k][0][0]] * orders[k][1][1]

        def far(self, way):
            return self.place if way == 0 else self.length - 1 - self.place

        def real(self, way, block):
            return block if way == 0 else self.length - 1 - block

        def block(self, way, block):
            return pl.ds(self.real(way, block) * self.units, self.units)

        def held(self, way, block):
            return self.gathered.at[pl.ds(self.base + self.real(way, block) * self.units, self.units)]

        def next(self, way):
            return me + self.step if way == 0 else me - self.step

        def copy(self, tick, way, src, dst):
            return copy(self.k, self.stage, tick, way, src, dst, self.next(way))

        def arrived(self, tick, way):
            if self.stage < 3:
                ref = self.landed.at[way, tick]
            else:
                ref = self.held(way, self.far(way) - 1 - tick)
            self.copy(tick, way, ref, ref).wait_recv()

        def begin(self):
            for way in (0, 1):
                far = self.far(way)
                if self.stage < 3:

                    @pl.when(far == 0)
                    def _():
                        for tick in range(self.length - 1):
                            src = self.source.at[self.block(way, self.length - 1 - tick)]
                            self.copy(tick, way, src, self.landed.at[way, tick]).start()
                else:

                    @pl.when(far < self.length - 1)
                    def _():
                        own = self.held(way, far)
                        self.copy(0, way, own, own).start()

        def reduce(self, tick, out):
            last = self.length - 2
            if tick < last:
                for way in (0, 1):
                    far = self.far(way)

                    @pl.when((far >= 1) & (far <= tick + 1))
                    def _():
                        self.arrived(tick, way)
                        here = self.landed.at[way, tick]
                        here[...] += self.source[self.block(way, last - tick + far)]
                        self.copy(tick + 1, way, here, self.landed.at[way, tick + 1]).start()
                return
            mine = pl.ds(self.place * self.units, self.units)

            @pl.when(self.place == 0)
            def _():
                self.arrived(last, 1)
                out[...] = self.source[mine] + self.landed[1, last]

            @pl.when(self.place == self.length - 1)
            def _():
                self.arrived(last, 0)
                out[...] = self.source[mine] + self.landed[0, last]

            if self.length > 2:

                @pl.when((self.place > 0) & (self.place < self.length - 1))
                def _():
                    self.arrived(last, 0)
                    self.arrived(last, 1)
                    out[...] = self.source[mine] + self.landed[0, last] + self.landed[1, last]

        def gather(self, tick):
            for way in (0, 1):
                far = self.far(way)

                @pl.when(far >= 1 + tick)
                def _():
                    self.arrived(tick, way)
                    if tick < self.length - 2:

                        @pl.when(far < self.length - 1)
                        def _():
                            got = self.held(way, far - 1 - tick)
                            self.copy(tick + 1, way, got, got).start()

        def sent(self):
            for way in (0, 1):
                far = self.far(way)
                for tick in range(self.length - 1):
                    if self.stage < 3:
                        ref, did = self.landed.at[way, tick], far <= tick
                    else:
                        ref, did = self.held(way, far - tick), far >= tick

                    @pl.when(did & (far < self.length - 1))
                    def _():
                        self.copy(tick, way, ref, ref).wait_send()

    def position(k, pair):
        where = (pair // fast, pair % fast)
        (first, _), (second, length) = orders[k]
        return where[first] * length + where[second]

    for k, stage, tick in arrivals:
        landed0, sums, landed1, middle, landed2, gathered = buffers[k]
        if stage == -1:
            for load in loads(k):
                load.wait()
            adam(k)
            core_copy(k, 0).start()
        elif stage == 0:
            core_copy(k, 0).wait_recv()
            for pair in range(n // 2):
                sums[position(k, pair)] = x_ref[pair, core, :, columns(k)] + landed0[pair]
            Line(k, 1).begin()
        elif stage == 5:
            core_copy(k, 5).wait_recv()
        else:
            line = Line(k, stage)
            last = tick == line.length - 2
            if stage == 1:
                line.reduce(tick, middle)
            elif stage == 2:
                own = gathered.at[pl.ds(line.base + line.place, 1)]
                line.reduce(tick, own)
                if last:
                    average = own[0] / n
                    slow_part = slow_ref[:, columns(k)]
                    synced = slow_part + blend_rate * (average - slow_part)
                    synced_ref[:, columns(k)] = synced
                    own[0] = synced
            else:
                line.gather(tick)
            if last and stage < 4:
                Line(k, stage + 1).begin()
            elif last:
                for pair in range(n // 2):
                    fresh_ref[pair, core, :, columns(k)] = gathered[position(k, pair)]
                core_copy(k, 5).start()

    for k in range(chunks):
        core_copy(k, 0).wait_send()
        for stage in (1, 2, 3, 4):
            Line(k, stage).sent()
        core_copy(k, 5).wait_send()


def synchronise(n, fast_weights, gradient, first_moment, second_moment, slow_weights):
    _, rows, cols = fast_weights.shape
    own = rows // n
    width = 128
    chunks = cols // width
    orders, arrivals = plan(n, chunks)
    slow, fast = grid_of(n)
    ticks = max(slow, fast) - 1
    f32 = jnp.float32
    buffers = []
    for (_, first), (_, second) in orders:
        buffers += [
            pltpu.VMEM((n // 2, own, width), f32),
            pltpu.VMEM((n // 2, own, width), f32),
            pltpu.VMEM((2, first - 1, second, own, width), f32),
            pltpu.VMEM((second, own, width), f32),
            pltpu.VMEM((2, second - 1, 1, own, width), f32),
            pltpu.VMEM((n // 2, own, width), f32),
        ]
    blocks = (n // 2, 2, own, cols)
    fresh, synced, new_first, new_second = pl.pallas_call(
        functools.partial(sync_kernel, n, chunks, orders, arrivals),
        out_shape=(
            pltpu.VMEM(blocks, f32),
            jax.ShapeDtypeStruct((own, cols), f32),
            pltpu.VMEM(blocks, f32),
            pltpu.VMEM(blocks, f32),
        ),
        in_specs=[pl.BlockSpec(memory_space=pl.ANY)] * 4 + [pl.BlockSpec(memory_space=pltpu.VMEM)],
        out_specs=[pl.BlockSpec(memory_space=pltpu.VMEM)] * 4,
        scratch_shapes=[
            pltpu.VMEM(blocks, f32),
            pltpu.VMEM(blocks, jnp.bfloat16),
            pltpu.SemaphoreType.DMA((chunks, 4)),
            pltpu.SemaphoreType.DMA((chunks, 6, ticks, 2)),
            pltpu.SemaphoreType.DMA((chunks, 6, ticks, 2)),
            *buffers,
        ],
        compiler_params=pltpu.CompilerParams(
            collective_id=0, has_side_effects=True, vmem_limit_bytes=36 * 2**20
        ),
        name="sync",
    )(*(array.reshape(blocks) for array in (fast_weights, gradient, first_moment, second_moment)), slow_weights)
    whole = fast_weights.shape
    return fresh.reshape(rows, cols), synced, new_first.reshape(whole), new_second.reshape(whole)


def solution(mesh):
    return jax.shard_map(
        functools.partial(synchronise, mesh.shape["dp"]),
        mesh=mesh,
        in_specs=(
            P("dp", None, "shard"),
            P("dp", None, "shard"),
            P("dp", None, "shard"),
            P("dp", None, "shard"),
            P("dp", "shard"),
        ),
        out_specs=(
            P(None, "shard"),
            P("dp", "shard"),
            P("dp", None, "shard"),
            P("dp", None, "shard"),
        ),
        check_vma=False,
    )
```

```python
import functools
import heapq

import jax
import jax.numpy as jnp
from jax import lax
from jax.experimental import pallas as pl
from jax.experimental.pallas import tpu as pltpu
from jax.sharding import PartitionSpec as P

beta_first = 0.9
beta_second = 0.999
learning_rate = 0.01
weight_decay = 0.05
epsilon = 1e-08
blend_rate = 0.5
first_bias = 1.0 - 0.9**5
second_bias = 1.0 - 0.999**5


def grid_of(n):
    chips = n // 2
    fast = 2 ** ((chips.bit_length() - 1) // 2)
    return chips // fast, fast


def plan(n, chunks):
    slow, fast = grid_of(n)
    orders = [((1, fast), (0, slow))] * chunks
    free, queued, events, arrivals = {}, {}, [], []

    def send(now, link, units):
        free[link] = max(now, free.get(link, 0.0)) + units * (0.15 if link == "core" else 0.9)
        return free[link]

    def line_of(k, stage):
        at = stage - 1 if stage < 3 else 4 - stage
        return orders[k][at] + (orders[k][1][1] if at == 0 else 1,)

    def start(now, k, stage, tick):
        if stage in (0, 5):
            done = send(now, "core", n // 2)
        else:
            axis, length, units = line_of(k, stage)
            if stage < 3:
                if tick == 0:
                    queued[k, stage] = [send(now, (axis, 0), units) for _ in range(length - 1)]
                ends = [queued[k, stage][tick]] + [send(now, (axis, i), units) for i in range(1, tick + 1)]
            else:
                ends = [send(now, (axis, i), units) for i in range(tick, length - 1)]
            done = max(ends)
        heapq.heappush(events, (done + 1.8, k, stage, tick))

    for k in range(chunks):
        heapq.heappush(events, (2.0 + 2.0 * k, k, -1, 0))
    while events:
        now, k, stage, tick = heapq.heappop(events)
        arrivals.append((k, stage, tick))
        last = stage in (-1, 0, 5) or tick == line_of(k, stage)[1] - 2
        if not last:
            start(now + 0.1, k, stage, tick + 1)
        elif stage < 5:
            start(now + 0.2, k, stage + 1, 0)
    return orders, arrivals


def sync_kernel(n, chunks, orders, arrivals, fast_hbm, grad_hbm, first_hbm, second_hbm, slow_ref, fresh_ref, synced_ref, first_ref, second_ref, *scratch):
    x_ref, grad_ref, load_sem, send_sem, recv_sem = scratch[:5]
    buffers = [scratch[5 + 6 * k : 11 + 6 * k] for k in range(chunks)]
    width = x_ref.shape[-1] // chunks
    slow, fast = grid_of(n)
    me = lax.axis_index("dp")
    core = me % 2
    places = (me // (2 * fast), (me // 2) % fast)
    strides = (2 * fast, 2)
    other = me + 1 - 2 * core

    def columns(k):
        return pl.ds(k * width, width)

    pairs = ((grad_hbm, grad_ref), (first_hbm, first_ref), (second_hbm, second_ref), (fast_hbm, x_ref))

    def loads(k):
        return [
            pltpu.make_async_copy(src.at[:, :, :, columns(k)], dst.at[:, :, :, columns(k)], load_sem.at[k, i])
            for i, (src, dst) in enumerate(pairs)
        ]

    def adam(k):
        @pl.loop(0, n)
        def _(block):
            at = (block // 2, block % 2, slice(None), columns(k))
            grad_value = grad_ref[at].astype(jnp.float32)
            new_first = beta_first * first_ref[at] + (1.0 - beta_first) * grad_value
            new_second = beta_second * second_ref[at] + (1.0 - beta_second) * grad_value * grad_value
            first_ref[at] = new_first
            second_ref[at] = new_second
            direction = new_first / first_bias / (jnp.sqrt(new_second / second_bias) + epsilon)
            weights = x_ref[at]
            x_ref[at] = weights - learning_rate * (direction + weight_decay * weights)

    for k in range(chunks):
        for load in loads(k):
            load.start()

    barrier = pltpu.get_barrier_semaphore()

    def greet(device):
        pl.semaphore_signal(barrier, inc=1, device_id={"dp": device}, device_id_type=pl.DeviceIdType.MESH)

    greet(other)
    peers = 1
    for axis, length in enumerate((slow, fast)):
        below, above = places[axis] > 0, places[axis] < length - 1
        pl.when(below)(functools.partial(greet, me - strides[axis]))
        pl.when(above)(functools.partial(greet, me + strides[axis]))
        peers = peers + jnp.where(below, 1, 0) + jnp.where(above, 1, 0)
    pl.semaphore_wait(barrier, peers)

    def copy(k, stage, tick, way, src, dst, device):
        return pltpu.make_async_remote_copy(
            src_ref=src,
            dst_ref=dst,
            send_sem=send_sem.at[k, stage, tick, way],
            recv_sem=recv_sem.at[k, stage, tick, way],
            device_id={"dp": device},
            device_id_type=pl.DeviceIdType.MESH,
        )

    def core_copy(k, stage):
        if stage == 0:
            src, dst = x_ref.at[:, 1 - core, :, columns(k)], buffers[k][0]
        else:
            src = dst = fresh_ref.at[:, core, :, columns(k)]
        return copy(k, stage, 0, 0, src, dst, other)

    class Line:
        def __init__(self, k, stage):
            at = stage - 1 if stage < 3 else 4 - stage
            self.k, self.stage = k, stage
            axis, self.length = orders[k][at]
            self.place = places[axis]
            self.units = orders[k][1][1] if at == 0 else 1
            self.step = strides[axis]
            landed0, sums, landed1, middle, landed2, gathered = buffers[k]
            self.source = sums if at == 0 else middle
            self.landed = landed1 if at == 0 else landed2
            self.gathered = gathered
            self.base = 0 if at == 0 else places[orders[k][0][0]] * orders[k][1][1]

        def far(self, way):
            return self.place if way == 0 else self.length - 1 - self.place

        def real(self, way, block):
            return block if way == 0 else self.length - 1 - block

        def block(self, way, block):
            return pl.ds(self.real(way, block) * self.units, self.units)

        def held(self, way, block):
            return self.gathered.at[pl.ds(self.base + self.real(way, block) * self.units, self.units)]

        def next(self, way):
            return me + self.step if way == 0 else me - self.step

        def copy(self, tick, way, src, dst):
            return copy(self.k, self.stage, tick, way, src, dst, self.next(way))

        def arrived(self, tick, way):
            if self.stage < 3:
                ref = self.landed.at[way, tick]
            else:
                ref = self.held(way, self.far(way) - 1 - tick)
            self.copy(tick, way, ref, ref).wait_recv()

        def begin(self):
            for way in (0, 1):
                far = self.far(way)
                if self.stage < 3:

                    @pl.when(far == 0)
                    def _():
                        for tick in range(self.length - 1):
                            src = self.source.at[self.block(way, self.length - 1 - tick)]
                            self.copy(tick, way, src, self.landed.at[way, tick]).start()
                else:

                    @pl.when(far < self.length - 1)
                    def _():
                        own = self.held(way, far)
                        self.copy(0, way, own, own).start()

        def reduce(self, tick, out):
            last = self.length - 2
            if tick < last:
                for way in (0, 1):
                    far = self.far(way)

                    @pl.when((far >= 1) & (far <= tick + 1))
                    def _():
                        self.arrived(tick, way)
                        here = self.landed.at[way, tick]
                        here[...] += self.source[self.block(way, last - tick + far)]
                        self.copy(tick + 1, way, here, self.landed.at[way, tick + 1]).start()
                return
            mine = pl.ds(self.place * self.units, self.units)

            @pl.when(self.place == 0)
            def _():
                self.arrived(last, 1)
                out[...] = self.source[mine] + self.landed[1, last]

            @pl.when(self.place == self.length - 1)
            def _():
                self.arrived(last, 0)
                out[...] = self.source[mine] + self.landed[0, last]

            if self.length > 2:

                @pl.when((self.place > 0) & (self.place < self.length - 1))
                def _():
                    self.arrived(last, 0)
                    self.arrived(last, 1)
                    out[...] = self.source[mine] + self.landed[0, last] + self.landed[1, last]

        def gather(self, tick):
            for way in (0, 1):
                far = self.far(way)

                @pl.when(far >= 1 + tick)
                def _():
                    self.arrived(tick, way)
                    if tick < self.length - 2:

                        @pl.when(far < self.length - 1)
                        def _():
                            got = self.held(way, far - 1 - tick)
                            self.copy(tick + 1, way, got, got).start()

        def sent(self):
            for way in (0, 1):
                far = self.far(way)
                for tick in range(self.length - 1):
                    if self.stage < 3:
                        ref, did = self.landed.at[way, tick], far <= tick
                    else:
                        ref, did = self.held(way, far - tick), far >= tick

                    @pl.when(did & (far < self.length - 1))
                    def _():
                        self.copy(tick, way, ref, ref).wait_send()

    def position(k, pair):
        where = (pair // fast, pair % fast)
        (first, _), (second, length) = orders[k]
        return where[first] * length + where[second]

    for k, stage, tick in arrivals:
        landed0, sums, landed1, middle, landed2, gathered = buffers[k]
        if stage == -1:
            for load in loads(k):
                load.wait()
            adam(k)
            core_copy(k, 0).start()
        elif stage == 0:
            core_copy(k, 0).wait_recv()
            for pair in range(n // 2):
                sums[position(k, pair)] = x_ref[pair, core, :, columns(k)] + landed0[pair]
            Line(k, 1).begin()
        elif stage == 5:
            core_copy(k, 5).wait_recv()
        else:
            line = Line(k, stage)
            last = tick == line.length - 2
            if stage == 1:
                line.reduce(tick, middle)
            elif stage == 2:
                own = gathered.at[pl.ds(line.base + line.place, 1)]
                line.reduce(tick, own)
                if last:
                    average = own[0] / n
                    slow_part = slow_ref[:, columns(k)]
                    synced = slow_part + blend_rate * (average - slow_part)
                    synced_ref[:, columns(k)] = synced
                    own[0] = synced
            else:
                line.gather(tick)
            if last and stage < 4:
                Line(k, stage + 1).begin()
            elif last:
                for pair in range(n // 2):
                    fresh_ref[pair, core, :, columns(k)] = gathered[position(k, pair)]
                core_copy(k, 5).start()

    for k in range(chunks):
        core_copy(k, 0).wait_send()
        for stage in (1, 2, 3, 4):
            Line(k, stage).sent()
        core_copy(k, 5).wait_send()


def synchronise(n, fast_weights, gradient, first_moment, second_moment, slow_weights):
    _, rows, cols = fast_weights.shape
    own = rows // n
    width = 256 if cols % 256 == 0 else 128
    chunks = cols // width
    orders, arrivals = plan(n, chunks)
    slow, fast = grid_of(n)
    ticks = max(slow, fast) - 1
    f32 = jnp.float32
    buffers = []
    for (_, first), (_, second) in orders:
        buffers += [
            pltpu.VMEM((n // 2, own, width), f32),
            pltpu.VMEM((n // 2, own, width), f32),
            pltpu.VMEM((2, first - 1, second, own, width), f32),
            pltpu.VMEM((second, own, width), f32),
            pltpu.VMEM((2, second - 1, 1, own, width), f32),
            pltpu.VMEM((n // 2, own, width), f32),
        ]
    blocks = (n // 2, 2, own, cols)
    fresh, synced, new_first, new_second = pl.pallas_call(
        functools.partial(sync_kernel, n, chunks, orders, arrivals),
        out_shape=(
            pltpu.VMEM(blocks, f32),
            jax.ShapeDtypeStruct((own, cols), f32),
            pltpu.VMEM(blocks, f32),
            pltpu.VMEM(blocks, f32),
        ),
        in_specs=[pl.BlockSpec(memory_space=pl.ANY)] * 4 + [pl.BlockSpec(memory_space=pltpu.VMEM)],
        out_specs=[pl.BlockSpec(memory_space=pltpu.VMEM)] * 4,
        scratch_shapes=[
            pltpu.VMEM(blocks, f32),
            pltpu.VMEM(blocks, jnp.bfloat16),
            pltpu.SemaphoreType.DMA((chunks, 4)),
            pltpu.SemaphoreType.DMA((chunks, 6, ticks, 2)),
            pltpu.SemaphoreType.DMA((chunks, 6, ticks, 2)),
            *buffers,
        ],
        compiler_params=pltpu.CompilerParams(
            collective_id=0, has_side_effects=True, vmem_limit_bytes=36 * 2**20
        ),
        name="sync",
    )(*(array.reshape(blocks) for array in (fast_weights, gradient, first_moment, second_moment)), slow_weights)
    whole = fast_weights.shape
    return fresh.reshape(rows, cols), synced, new_first.reshape(whole), new_second.reshape(whole)


def solution(mesh):
    return jax.shard_map(
        functools.partial(synchronise, mesh.shape["dp"]),
        mesh=mesh,
        in_specs=(
            P("dp", None, "shard"),
            P("dp", None, "shard"),
            P("dp", None, "shard"),
            P("dp", None, "shard"),
            P("dp", "shard"),
        ),
        out_specs=(
            P(None, "shard"),
            P("dp", "shard"),
            P("dp", None, "shard"),
            P("dp", None, "shard"),
        ),
        check_vma=False,
    )
```
